32 devices in a mesh: groups: 2 (over y), seq: 4 (over z), section: 2 (over x), tp: 2 (over core).
Axes of the slice: x: 2, y: 2, z: 4, core: 2. Of those that a mesh axis runs over, the one named last changes fastest.
Arguments:
- qkv: bfloat16 [4, 1024, 3, 2048], P(('groups', 'section'), ('seq', 'tp')), parts along dimension 0, may hold values from -100 to 100
- stream: bfloat16 [4, 1024, 3072], P(('groups', 'section'), ('seq', 'tp')), parts along dimension 0, may hold values from -6 to 6
- out_weight: bfloat16 [2048, 3072], P('tp'), may hold values from -0.125 to 0.125
- mod_scale: float32 [4, 3072], P(('groups', 'section')), parts along dimension 0, may hold values from -3 to 3
- mod_shift: float32 [4, 3072], P(('groups', 'section')), parts along dimension 0, may hold values from -3 to 3
- final_weight: bfloat16 [3072, 64], replicated, may hold values from -0.109375 to 0.109375
- latent: float32 [4, 1024, 64], P(('groups', 'section'), ('seq', 'tp')), parts along dimension 0, may hold values from -6 to 6
- step_size: float32 [4], P(('groups', 'section')), parts along dimension 0, may hold values from 0.2 to 1
- frame_counts: int32 [4, 4], P(('groups', 'section')), parts along dimension 0, may hold values from 1 to 4, 8 in all within a row
- finished: int32 [4, 4], P(('groups', 'section')), parts along dimension 0, may hold values 0 or 1
- conv_weight: bfloat16 [3, 3, 3, 16, 512], P(None, None, None, None, 'tp'), may hold values from -0.3125 to 0.3125
- conv_bias: float32 [512], P('tp'), may hold values from -3 to 3
- up_weight: bfloat16 [512, 512], P('tp'), may hold values from -0.25 to 0.25
- up_bias: float32 [512], P('tp'), may hold values from -3 to 3
Outputs:
- new_latent: float32 [4, 1024, 64], P(('groups', 'section'), ('seq', 'tp')), parts along dimension 0
- decoded: bfloat16 [4, 8, 16, 32, 512], P(('groups', 'section'), None, 'seq', None, 'tp'), parts along dimension 0
The draws below stay inside these ranges and needn't reach their ends.
There are 2 independent parts, one for each index of `groups`. The reference program is written for one: setup_inputs(seed, part) draws one part's arguments, and reference() takes and returns one part's arrays. A program takes and returns all parts, laid end to end along the dimension named above; an argument that names none is the same for every part. Nothing has to cross between parts.
Inputs may be any that keep to these rules, and one draw needn't show every extreme that they name: `frame_counts`: a part's 4 requests are packed in order and their frame counts sum to 8.
All inputs are finite; a program needn't handle non-finite values. No bound on the sum of `finished` on one device may be relied on, other than what follows from the above.
Results may differ from the reference program's by a relative error of at most 0.012.
Values may be sent and summed in bfloat16 or wider, within the bound.
No kernel may reach another device: no remote copies, remote signals or barrier semaphores. Data moves between devices by JAX's collectives and lax.ppermute only.
A program may use at most 64 MiB of HBM per device.

```python
import math
import jax
import jax.numpy as jnp
import numpy as np
from jax import lax

D = 3072
HEADS = 16
HD = 128
LATC = 16
PATCH = 64
VAEC = 512
UPC = 512
PROWS = 8
PCOLS = 16
REQ = 4
F_TOK = 128
LROWS = 16
LCOLS = 32
FRAMES = 8
TOKS = 1024
MAXF = 4
N_SECTION = 2


def draw_qkv(key, part):
    array_dims = (N_SECTION, TOKS, 3, HEADS * HD)
    base = jnp.clip(jax.random.normal(key, array_dims, jnp.float32), -4.0, 4.0)
    return base.astype(jnp.bfloat16)


def with_ends(entries, key, smallest, high):
    index_at = [jax.random.randint(jax.random.fold_in(key, axis), (), 0, length) for axis, length in enumerate(entries.shape)]
    longest = entries.shape.index(max(entries.shape))
    neighbour = index_at[:longest] + [(index_at[longest] + 1) % entries.shape[longest]] + index_at[longest + 1:]
    return entries.at[tuple(index_at)].set(smallest).at[tuple(neighbour)].set(high)


def level_of(rng, shape, split, least, high):
    gain, own = 1.0, jax.random.fold_in(rng, 6)
    for position, parts in split:
        heights = jnp.exp(jax.random.uniform(jax.random.fold_in(own, position), (parts,), jnp.float32, least / len(split), high / len(split)))
        gain = gain * jnp.repeat(heights, shape[position] // parts).reshape([-1 if axis == position else 1 for axis in range(len(shape))])
    return gain


def profile(amount, total, bound, lean):
    weights = [(1 << 20) // math.isqrt(rank ** lean) + 1 for rank in range(2, amount + 1)]
    surplus, given = total - bound - (amount - 1), [1] * (amount - 1)
    while surplus > 0:
        free = [i for i in range(amount - 1) if given[i] < bound]
        whole, budget = sum([weights[i] for i in free]), surplus
        for i in free:
            extra = min(bound - given[i], max(1, budget * weights[i] // whole), surplus)
            given[i] = given[i] + extra
            surplus = surplus - extra
    return np.array([bound] + given)


def uneven_parts(key, number_of, total, reach, lean):
    if number_of == 2:
        one = jax.random.randint(key, (), max(1, total - reach), min(reach, total - 1) + 1)
        return jnp.stack([one, total - one])
    tallies = jnp.asarray(profile(number_of, total, reach, lean), jnp.int32)
    twos = (number_of - 1) // 2
    giver, taker = tallies[1:1 + 2 * twos:2], tallies[2:2 + 2 * twos:2]
    room = jnp.minimum(giver - 1, reach - taker)
    passed = jax.random.randint(jax.random.fold_in(key, 1), (twos,), 0, 1 << 20) % (room + 1)
    tallies = tallies.at[1:1 + 2 * twos:2].set(giver - passed).at[2:2 + 2 * twos:2].set(taker + passed)
    return tallies[jax.random.permutation(jax.random.fold_in(key, 2), number_of)]


def scatter_about(stream_key, shape, spread, reach, cuts=(), held_as=jnp.bfloat16):
    drawn = jax.random.normal(stream_key, shape, jnp.float32) * spread
    if len(cuts) > 0:
        drawn = level_of(stream_key, shape, cuts, -0.22, 0.18) * drawn
    return jnp.clip(drawn, min=-reach, max=reach).astype(held_as)


def setup_inputs(seed: int = 0, part: int = 0) -> dict:
    key_of = jax.random.split(jax.random.key(seed), 15)
    part_keys = jax.random.split(jax.random.fold_in(key_of[14], part), 15)
    return {
        "qkv": draw_qkv(jax.random.fold_in(jax.random.fold_in(key_of[14], part), 71), part),
        "stream": scatter_about(part_keys[1], (N_SECTION, TOKS, D), 1.0, 6.0, ((0, 2), (1, 8))),
        "out_weight": scatter_about(key_of[2], (HEADS * HD, D), (HEADS * HD) ** -0.5, 0.125, ((0, 2),)),
        "mod_scale": scatter_about(part_keys[3], (N_SECTION, D), 0.5, 3.0, ((0, 2),), jnp.float32),
        "mod_shift": scatter_about(part_keys[4], (N_SECTION, D), 0.5, 3.0, ((0, 2),), jnp.float32),
        "final_weight": scatter_about(key_of[5], (D, PATCH), D ** -0.5, 0.109375),
        "latent": scatter_about(part_keys[6], (N_SECTION, TOKS, PATCH), 1.0, 6.0, ((0, 2), (1, 8)), jnp.float32),
        "step_size": jnp.clip(0.2 + 0.8 * jax.random.uniform(part_keys[7], (N_SECTION,), jnp.float32) ** level_of(part_keys[7], (N_SECTION,), ((0, 2),), -0.2, 0.2), 0.2, 1.0),
        "frame_counts": jax.vmap(lambda own: uneven_parts(own, REQ, FRAMES, MAXF, 2))(jax.random.split(part_keys[8], N_SECTION)).reshape((N_SECTION, REQ)).astype(jnp.int32),
        "finished": with_ends((jax.random.randint(part_keys[9], (N_SECTION, REQ), 0, 2) < 1).astype(jnp.int32), jax.random.fold_in(part_keys[9], 1), 0, 1),
        "conv_weight": scatter_about(key_of[10], (3, 3, 3, LATC, VAEC), (27 * LATC) ** -0.5, 0.3125, ((4, 2),)),
        "conv_bias": scatter_about(key_of[11], (VAEC,), 0.5, 3.0, ((0, 2),), jnp.float32),
        "up_weight": scatter_about(key_of[12], (VAEC, UPC), VAEC ** -0.5, 0.25, ((0, 2),)),
        "up_bias": scatter_about(key_of[13], (UPC,), 0.5, 3.0, ((0, 2),), jnp.float32),
    }


EPSILON = 1e-06

def request_index(positions, counts, unit):
    ends = jnp.cumsum(counts) * unit
    return lax.optimization_barrier(jnp.sum((positions[:, None] >= ends[None, :]).astype(jnp.int32), axis=1))

def attend_section(packed, requests):
    tokens = packed.shape[0]
    block = math.gcd(tokens, 512)
    score_scale = 1.0 / math.sqrt(HD)
    query_heads = jnp.moveaxis(packed[:, 0], 1, 0)
    key_heads = jnp.moveaxis(packed[:, 1], 1, 0)
    value_heads = jnp.moveaxis(packed[:, 2], 1, 0)

    def head_attention(head_trio):
        queries, key_rows, value_rows = head_trio

        def block_attention(block_pair):
            query_rows, query_req = block_pair
            scores = jnp.dot(query_rows, key_rows.T, preferred_element_type=jnp.float32) * score_scale
            allowed = query_req[:, None] == requests[None, :]
            largest = lax.optimization_barrier(jnp.max(jnp.where(allowed, scores, -jnp.inf), axis=1))
            weights = jnp.where(allowed, jnp.exp(scores - largest[:, None]), 0.0)
            weight_sum = lax.optimization_barrier(jnp.sum(weights, axis=1))
            product = jnp.dot(weights.astype(jnp.bfloat16), value_rows, preferred_element_type=jnp.float32)
            return (product / weight_sum[:, None]).astype(jnp.bfloat16)
        blocks = lax.map(block_attention, (queries.reshape(-1, block, HD), requests.reshape(-1, block)))
        return blocks.reshape(tokens, HD)
    heads = lax.map(head_attention, (query_heads, key_heads, value_heads))
    return jnp.moveaxis(heads, 0, 1).reshape(tokens, HEADS * HD)

def decode_frames(frames_video, counts, done_flags, conv_weight, conv_bias, up_weight, up_bias):
    frame_ids = jnp.arange(FRAMES, dtype=jnp.int32)
    owner_req = request_index(frame_ids, counts, 1)
    starts = jnp.cumsum(counts) - counts
    selector = owner_req[:, None] == jnp.arange(REQ, dtype=jnp.int32)[None, :]
    first_frame = lax.optimization_barrier(jnp.sum(jnp.where(selector, starts[None, :], 0), axis=1))
    alive_frame = lax.optimization_barrier(jnp.sum(jnp.where(selector, done_flags[None, :], 0), axis=1))
    padded = jnp.pad(frames_video, ((2, 0), (1, 1), (1, 1), (0, 0)))
    columns_list = []
    for time_tap in range(3):
        inside = frame_ids - 2 + time_tap >= first_frame
        for row_tap in range(3):
            for col_tap in range(3):
                window = padded[time_tap:time_tap + FRAMES, row_tap:row_tap + LROWS, col_tap:col_tap + LCOLS]
                columns_list.append(jnp.where(inside[:, None, None, None], window, jnp.zeros_like(window)))
    stacked = jnp.concatenate(columns_list, axis=3).reshape(-1, 27 * LATC)
    kernel = conv_weight.reshape(27 * LATC, VAEC)
    hidden = jax.nn.silu(jnp.dot(stacked, kernel, preferred_element_type=jnp.float32) + conv_bias).astype(jnp.bfloat16)
    upsampled = jnp.dot(hidden, up_weight, preferred_element_type=jnp.float32) + up_bias
    upsampled = upsampled.reshape(FRAMES, LROWS, LCOLS, UPC) * alive_frame.astype(jnp.float32)[:, None, None, None]
    return upsampled.astype(jnp.bfloat16)

def reference(qkv, stream, out_weight, mod_scale, mod_shift, final_weight, latent, step_size, frame_counts, finished, conv_weight, conv_bias, up_weight, up_bias):
    positions = jnp.arange(TOKS, dtype=jnp.int32)
    latent_list = []
    video_list = []
    for section_index in range(N_SECTION):
        counts = frame_counts[section_index]
        requests = request_index(positions // F_TOK, counts, 1)
        packed = qkv[section_index].reshape(TOKS, 3, HEADS, HD)
        attended = attend_section(packed, requests)
        mixed_stream = stream[section_index].astype(jnp.float32) + jnp.dot(attended, out_weight, preferred_element_type=jnp.float32)
        average = lax.optimization_barrier(jnp.mean(mixed_stream, axis=1, keepdims=True))
        centred = mixed_stream - average
        variance = lax.optimization_barrier(jnp.mean(centred * centred, axis=1, keepdims=True))
        normed = centred / jnp.sqrt(variance + EPSILON)
        modulated = (normed * (1.0 + mod_scale[section_index]) + mod_shift[section_index]).astype(jnp.bfloat16)
        velocity = jnp.dot(modulated, final_weight, preferred_element_type=jnp.float32)
        updated = latent[section_index] + step_size[section_index] * velocity
        latent_list.append(updated)
        frames_video = updated.reshape(FRAMES, PROWS, PCOLS, 2, 2, LATC).transpose(0, 1, 3, 2, 4, 5)
        frames_video = frames_video.reshape(FRAMES, LROWS, LCOLS, LATC).astype(jnp.bfloat16)
        video_list.append(decode_frames(frames_video, counts, finished[section_index], conv_weight, conv_bias, up_weight, up_bias))
    return (jnp.stack(latent_list), jnp.stack(video_list))
```

```python
import functools
import math

import jax
import jax.numpy as jnp
from jax import lax
from jax.experimental import pallas as pl
from jax.experimental.pallas import tpu as pltpu
from jax.sharding import PartitionSpec as P

HD = 128
F_TOK = 128
LATC = 16
PROWS = 8
PCOLS = 16
LROWS = 16
LCOLS = 32

EPSILON = 1e-06
NEG_FILL = -1e30
F32 = jnp.float32
BF16 = jnp.bfloat16
MIB = 1 << 20


VMEM = pl.BlockSpec(memory_space=pltpu.VMEM)
SMEM = pl.BlockSpec(memory_space=pltpu.SMEM)
ANY = pl.BlockSpec(memory_space=pl.ANY)


def request_of(frame, table, requests):
    end = table[0]
    found = (frame >= end).astype(jnp.int32)
    for j in range(1, requests):
        end = end + table[j]
        found = found + (frame >= end).astype(jnp.int32)
    return found


def same_request(frame, other, table, requests, frames):
    inside = jnp.logical_and(other >= 0, other < frames)
    same = request_of(other, table, requests) == request_of(frame, table, requests)
    return jnp.logical_and(inside, same)


def attend_block(q_ref, k_ref, v_ref, largest, total, acc_in, acc_out):
    heads = q_ref.shape[1] // HD
    lane = lax.broadcasted_iota(jnp.int32, largest.shape, 1)
    new_largest, new_total = largest, total
    for h in range(heads):
        cols = slice(h * HD, (h + 1) * HD)
        scores = lax.dot_general(
            q_ref[:, cols], k_ref[:, cols], (((1,), (1,)), ((), ())), preferred_element_type=F32
        ) * (1.0 / math.sqrt(HD))
        before = largest[:, h : h + 1]
        after = jnp.maximum(before, jnp.max(scores, axis=1, keepdims=True))
        weights = jnp.exp(scores - after)
        factor = jnp.exp(before - after)
        row_sum = total[:, h : h + 1] * factor + jnp.sum(weights, axis=1, keepdims=True)
        product = jnp.dot(weights.astype(BF16), v_ref[:, cols], preferred_element_type=F32)
        acc_out[:, cols] = acc_in[:, cols] * factor + product
        new_largest = jnp.where(lane == h, after, new_largest)
        new_total = jnp.where(lane == h, row_sum, new_total)
    return new_largest, new_total


def attend_kernel(offsets, requests, frames, table, qkv, *rest):
    sources = rest[: len(offsets) - 1]
    acc, largest, total, q_buf, kv_buf, q_sem, kv_sem = rest[len(offsets) - 1 :]
    mine, sign = table[requests], table[requests + 1]
    q_copy = pltpu.make_async_copy(qkv.at[0], q_buf, q_sem)
    q_copy.start()
    count = jnp.int32(0)
    for off, src in zip(offsets, (qkv.at[1:3],) + sources):
        wanted = same_request(mine, mine + off * sign, table, requests, frames)

        @pl.when(wanted)
        def _(src=src, slot=count):
            pltpu.make_async_copy(src, kv_buf.at[slot], kv_sem.at[slot]).start()

        count = count + wanted.astype(jnp.int32)
    acc[...] = jnp.zeros_like(acc)
    largest[...] = jnp.full(largest.shape, NEG_FILL, F32)
    total[...] = jnp.zeros_like(total)
    q_copy.wait()

    def step(i, carry):
        pltpu.make_async_copy(qkv.at[1:3], kv_buf.at[i], kv_sem.at[i]).wait()
        m, l = attend_block(
            q_buf, kv_buf.at[i, 0], kv_buf.at[i, 1], largest[...], total[...], acc, acc
        )
        largest[...] = m
        total[...] = l
        return carry

    lax.fori_loop(0, count, step, 0)


def finish_kernel(
    offset, requests, frames, seq, nrows,
    table, step_size, qkv, last, acc, largest, total, w_own, w_other, stream,
    scale, shift, fw, latent,
    new_latent, send,
    att, mixed, acc2, q_buf, kv_buf, sems,
):
    mine, sign, place = table[requests], table[requests + 1], table[requests + 2]
    wanted = same_request(mine, mine + offset * sign, table, requests, frames)
    heads = q_buf.shape[1] // HD
    half = heads // 2

    def store(source, row_sum):
        for h in range(heads):
            cols = slice(h * HD, (h + 1) * HD)
            inside = slice((h % half) * HD, (h % half + 1) * HD)
            att[h // half, :, inside] = (source[:, cols] / row_sum[:, h : h + 1]).astype(BF16)

    @pl.when(wanted)
    def _():
        q_copy = pltpu.make_async_copy(qkv.at[0], q_buf, sems.at[0])
        kv_copy = pltpu.make_async_copy(last, kv_buf, sems.at[1])
        q_copy.start()
        kv_copy.start()
        q_copy.wait()
        kv_copy.wait()
        _, row_sum = attend_block(
            q_buf, kv_buf.at[0], kv_buf.at[1], largest[...], total[...], acc, acc2
        )
        store(acc2, row_sum)

    @pl.when(jnp.logical_not(wanted))
    def _():
        store(acc, total[...])

    width = mixed.shape[1]
    tile = 512 if width % 512 == 0 else width
    rows = mixed.shape[0]

    def project(i, running):
        cols = pl.ds(pl.multiple_of(i * tile, tile), tile)
        value = (
            jnp.dot(att[place], w_own[:, cols], preferred_element_type=F32)
            + jnp.dot(att[1 - place], w_other[:, cols], preferred_element_type=F32)
            + stream[:, cols].astype(F32)
        )
        mixed[:, cols] = value
        return running + jnp.sum(value, axis=1, keepdims=True)

    summed = lax.fori_loop(0, width // tile, project, jnp.zeros((rows, 1), F32))
    average = summed * (1.0 / width)
    squares = jnp.zeros((rows, 1), F32)
    for i in range(width // tile):
        centred = mixed[:, i * tile : (i + 1) * tile] - average
        squares = squares + jnp.sum(centred * centred, axis=1, keepdims=True)
    inverse = 1.0 / jnp.sqrt(squares * (1.0 / width) + EPSILON)
    velocity = jnp.zeros(new_latent.shape, F32)
    for i in range(width // tile):
        cols = slice(i * tile, (i + 1) * tile)
        normed = (mixed[:, cols] - average) * inverse
        modulated = (normed * (1.0 + scale[:, cols]) + shift[:, cols]).astype(BF16)
        velocity = velocity + lax.dot_general(
            fw[:, cols], modulated, (((1,), (1,)), ((), ())), preferred_element_type=F32
        )
    updated = latent[...] + step_size[0] * velocity
    new_latent[...] = updated

    column = lax.broadcasted_iota(jnp.int32, (LATC, F_TOK), 1) % PCOLS
    pieces = []
    for i in range(2):
        even = updated[2 * i * LATC : (2 * i + 1) * LATC]
        odd = updated[(2 * i + 1) * LATC : (2 * i + 2) * LATC]
        pieces.append(jnp.where(column == 0, 0.0, pltpu.roll(odd, 1, 1)))
        pieces.append(even)
        pieces.append(odd)
        pieces.append(jnp.where(column == PCOLS - 1, 0.0, pltpu.roll(even, F_TOK - 1, 1)))
    spread = jnp.concatenate(pieces, axis=0).T
    lower = lax.broadcasted_iota(jnp.int32, (PCOLS, 8 * LATC), 1) < 4 * LATC
    blank = jnp.zeros((PCOLS, 8 * LATC), F32)
    patch = [spread[r * PCOLS : (r + 1) * PCOLS] for r in range(PROWS)]
    for s in range(seq):
        first = (s * LROWS // seq) // 2
        for k in range(nrows):
            send[s, k * PCOLS : (k + 1) * PCOLS, :] = patch[first + k].astype(BF16)
        below = patch[first + nrows] if first + nrows < PROWS else blank
        above = patch[first - 1] if first > 0 else blank
        edge = jnp.where(lower, below, above)
        send[s, nrows * PCOLS : (nrows + 1) * PCOLS, :] = edge.astype(BF16)


def arrange_kernel(own, other, out):
    out[...] = jnp.zeros_like(out)
    block = 4 * LATC
    outputs = own.shape[4]
    for parity in range(2):
        taps = ((0, 0, 1), (0, 1, 2), (1, 1, 0)) if parity == 0 else ((0, 0, 0), (0, 1, 1), (1, 0, 2))
        for a in range(3):
            for blk, half, b in taps:
                base = ((a * 2 + blk) * 2 + half) * block
                for jj in range(2):
                    for e in range(3):
                        rows = slice(base + (e + jj) * LATC, base + (e + jj + 1) * LATC)
                        at = jj * 2 * outputs
                        out[parity, rows, at : at + outputs] = own[a, b, e]
                        out[parity, rows, at + outputs : at + 2 * outputs] = other[a, b, e]


def decode_kernel(
    requests, frames, seq, slab, nrows,
    table, own, other, kernel, bias_own, bias_other, up_own, up_other, up_bias,
    out,
    video, lhs, up, pixels,
):
    place, row_place = table[2 * requests], table[2 * requests + 1]
    for s in range(seq):
        video[2 * s + place] = own[s]
        video[2 * s + 1 - place] = other[s]
    width = out.shape[3]
    hidden = up_own.shape[0]
    cols = pl.ds(pl.multiple_of(place * width, width), width)
    up[0:hidden] = up_own[:, cols]
    up[hidden : 2 * hidden] = up_other[:, cols]
    owner = [request_of(f, table, requests) for f in range(frames)]
    blank = jnp.zeros((PCOLS, 8 * LATC), BF16)

    def tile_of(frame, k):
        return video[frame, k * PCOLS : (k + 1) * PCOLS, :]

    parities = (0, 1) if slab % 2 == 0 else (None,)
    bias = jnp.concatenate([bias_own[...], bias_other[...]] * 2, axis=1)
    for group, parity in enumerate(parities):
        for f in range(frames):
            for k in range(nrows):
                rows = slice((f * nrows + k) * PCOLS, (f * nrows + k + 1) * PCOLS)
                if parity is None:
                    beside = nrows
                elif parity == 0:
                    beside = k - 1 if k > 0 else nrows
                else:
                    beside = k + 1
                for a in range(3):
                    g = f - 2 + a
                    for blk, k_in in enumerate((k, beside)):
                        at = (a * 2 + blk) * 8 * LATC
                        value = blank
                        if g >= 0:
                            value = tile_of(g, k_in)
                            if a < 2:
                                value = jnp.where(owner[g] == owner[f], value, blank)
                        lhs[group, rows, at : at + 8 * LATC] = value
        which = lax.rem(row_place, 2) if parity is None else parity
        dense = jnp.dot(lhs[group], kernel[which], preferred_element_type=F32) + bias
        act = (dense * (1.0 / (1.0 + jnp.exp(-dense)))).astype(BF16)
        for jj in range(2):
            part = act[:, jj * 2 * hidden : (jj + 1) * 2 * hidden]
            shared = jnp.dot(part, up[...], preferred_element_type=F32) + up_bias[...]
            for f in range(frames):
                alive = table[requests + owner[f]].astype(F32)
                for k in range(nrows):
                    rows = slice((f * nrows + k) * PCOLS, (f * nrows + k + 1) * PCOLS)
                    y = k if parity is None else 2 * k + parity
                    start = (f * slab + y) * LCOLS + jj
                    value = shared[rows] * alive
                    for lanes in range(width // HD):
                        at = slice(lanes * HD, (lanes + 1) * HD)
                        pixels[lanes, pl.ds(start, PCOLS, stride=2), :] = value[:, at]
    for f in range(frames):
        for y in range(slab):
            start = (f * slab + y) * LCOLS
            for lanes in range(width // HD):
                at = slice(lanes * HD, (lanes + 1) * HD)
                out[f, y, :, at] = pixels[lanes, start : start + LCOLS, :].astype(BF16)


def on_device(
    qkv,
    stream,
    out_weight,
    mod_scale,
    mod_shift,
    final_weight,
    latent,
    step_size,
    frame_counts,
    finished,
    conv_weight,
    conv_bias,
    up_weight,
    up_bias,
):
    seq, cores = lax.axis_size("seq"), lax.axis_size("tp")
    row_place, place = lax.axis_index("seq"), lax.axis_index("tp")
    tokens = qkv.shape[1]
    assert tokens == F_TOK and cores == 2
    requests = frame_counts.shape[1]
    frames = seq * cores
    reach = frames // 2 - 1
    hops = (reach - 1) // 2
    assert reach == 2 * hops + 1
    model = qkv.shape[3]
    both = ("seq", "tp")
    outward = [(2 * z + 1, 2 * z + 3) for z in range(seq - 1)]
    outward += [(2 * z + 2, 2 * z) for z in range(seq - 1)]
    inward = [(2 * z, 2 * z + 2) for z in range(seq - 1)]
    inward += [(2 * z + 3, 2 * z + 1) for z in range(seq - 1)]
    across = [(2 * z + 1, 2 * z + 2) for z in range(seq - 1)]
    across += [(2 * z + 2, 2 * z + 1) for z in range(seq - 1)]
    swap = [(0, 1), (1, 0)]

    stacked = qkv[0].transpose(1, 0, 2)
    pair = stacked[1:3]
    sources, offsets = [], [0]
    out_chain = in_chain = pair
    for h in range(1, hops + 1):
        out_chain = lax.ppermute(out_chain, both, outward)
        in_chain = lax.ppermute(in_chain, both, inward)
        if h == 1:
            sources.append(lax.ppermute(pair, "tp", swap))
            offsets.append(1)
        sources += [out_chain, lax.ppermute(out_chain, "tp", swap)]
        offsets += [2 * h, -(2 * h - 1)]
        sources += [in_chain, lax.ppermute(in_chain, "tp", swap)]
        offsets += [-2 * h, 2 * h + 1]
    last = lax.ppermute(out_chain, both, across)

    w_other = lax.ppermute(out_weight, "tp", swap)
    conv_other = lax.ppermute(conv_weight, "tp", swap)
    bias_other = lax.ppermute(conv_bias[None], "tp", swap)
    up_other = lax.ppermute(up_weight, "tp", swap)

    counts = frame_counts[0]
    table = jnp.concatenate(
        [counts, jnp.stack([row_place * 2 + place, 1 - 2 * place, place]).astype(jnp.int32)]
    )
    decode_table = jnp.concatenate(
        [counts, finished[0], jnp.stack([place, row_place]).astype(jnp.int32)]
    )

    slots = frames // 2
    acc, largest, total = pl.pallas_call(
        functools.partial(attend_kernel, tuple(offsets), requests, frames),
        name="attend",
        out_shape=(
            jax.ShapeDtypeStruct((tokens, model), F32),
            jax.ShapeDtypeStruct((tokens, HD), F32),
            jax.ShapeDtypeStruct((tokens, HD), F32),
        ),
        in_specs=[SMEM] + [ANY] * (1 + len(sources)),
        out_specs=(VMEM, VMEM, VMEM),
        scratch_shapes=[
            pltpu.VMEM((tokens, model), BF16),
            pltpu.VMEM((slots, 2, tokens, model), BF16),
            pltpu.SemaphoreType.DMA,
            pltpu.SemaphoreType.DMA((slots,)),
        ],
        compiler_params=pltpu.CompilerParams(vmem_limit_bytes=(slots + 8) * MIB),
    )(table, stacked, *sources)

    arranged = pl.pallas_call(
        arrange_kernel,
        name="arrange",
        out_shape=jax.ShapeDtypeStruct((2, 48 * LATC, 4 * conv_weight.shape[4]), BF16),
        in_specs=[VMEM, VMEM],
        out_specs=VMEM,
        compiler_params=pltpu.CompilerParams(vmem_limit_bytes=8 * MIB),
    )(conv_weight, conv_other)

    slab = LROWS // seq
    assert slab == 1 or slab % 2 == 0
    nrows = (slab + 1) // 2
    width = stream.shape[2]
    patch = final_weight.shape[1]
    new_latent, send = pl.pallas_call(
        functools.partial(finish_kernel, -reach, requests, frames, seq, nrows),
        name="finish",
        out_shape=(
            jax.ShapeDtypeStruct((patch, tokens), F32),
            jax.ShapeDtypeStruct((seq, (nrows + 1) * PCOLS, 8 * LATC), BF16),
        ),
        in_specs=[SMEM, SMEM, ANY, ANY] + [VMEM] * 10,
        out_specs=(VMEM, VMEM),
        scratch_shapes=[
            pltpu.VMEM((2, tokens, model // 2), BF16),
            pltpu.VMEM((tokens, width), F32),
            pltpu.VMEM((tokens, model), F32),
            pltpu.VMEM((tokens, model), BF16),
            pltpu.VMEM((2, tokens, model), BF16),
            pltpu.SemaphoreType.DMA((2,)),
        ],
        compiler_params=pltpu.CompilerParams(vmem_limit_bytes=32 * MIB),
    )(
        table,
        step_size,
        stacked,
        last,
        acc,
        largest,
        total,
        out_weight,
        w_other,
        stream[0],
        mod_scale,
        mod_shift,
        final_weight.T,
        latent[0].T,
    )

    received = lax.all_to_all(send, "seq", split_axis=0, concat_axis=0, tiled=True)
    received_other = lax.ppermute(received, "tp", swap)
    out_width = up_bias.shape[0]
    decoded = pl.pallas_call(
        functools.partial(decode_kernel, requests, frames, seq, slab, nrows),
        name="decode",
        out_shape=jax.ShapeDtypeStruct((frames, slab, LCOLS, out_width), BF16),
        in_specs=[SMEM] + [VMEM] * 8,
        out_specs=VMEM,
        scratch_shapes=[
            pltpu.VMEM((frames, (nrows + 1) * PCOLS, 8 * LATC), BF16),
            pltpu.VMEM((2 if slab % 2 == 0 else 1, frames * nrows * PCOLS, 48 * LATC), BF16),
            pltpu.VMEM((2 * up_weight.shape[0], out_width), BF16),
            pltpu.VMEM((out_width // HD, frames * slab * LCOLS, HD), F32),
        ],
        compiler_params=pltpu.CompilerParams(vmem_limit_bytes=24 * MIB),
    )(
        decode_table,
        received,
        received_other,
        arranged,
        conv_bias[None],
        bias_other,
        up_weight,
        up_other,
        up_bias[None],
    )
    return (new_latent.T[None], decoded[None])


def solution(mesh):
    in_specs = (
        P(("groups", "section"), ("seq", "tp"), None, None),
        P(("groups", "section"), ("seq", "tp"), None),
        P("tp", None),
        P(("groups", "section"), None),
        P(("groups", "section"), None),
        P(),
        P(("groups", "section"), ("seq", "tp"), None),
        P(("groups", "section")),
        P(("groups", "section"), None),
        P(("groups", "section"), None),
        P(None, None, None, None, "tp"),
        P("tp"),
        P("tp", None),
        P("tp"),
    )
    out_specs = (
        P(("groups", "section"), ("seq", "tp"), None),
        P(("groups", "section"), None, "seq", None, "tp"),
    )
    return jax.shard_map(
        on_device, mesh=mesh, in_specs=in_specs, out_specs=out_specs, check_vma=False
    )
```

```python
import functools
import math

import jax
import jax.numpy as jnp
from jax import lax
from jax.experimental import pallas as pl
from jax.experimental.pallas import tpu as pltpu
from jax.sharding import PartitionSpec as P

HD = 128
F_TOK = 128
LATC = 16
PROWS = 8
PCOLS = 16
LROWS = 16
LCOLS = 32

EPSILON = 1e-06
NEG_FILL = -1e30
F32 = jnp.float32
BF16 = jnp.bfloat16
MIB = 1 << 20


VMEM = pl.BlockSpec(memory_space=pltpu.VMEM)
SMEM = pl.BlockSpec(memory_space=pltpu.SMEM)
ANY = pl.BlockSpec(memory_space=pl.ANY)


def request_of(frame, table, requests):
    end = table[0]
    found = (frame >= end).astype(jnp.int32)
    for j in range(1, requests):
        end = end + table[j]
        found = found + (frame >= end).astype(jnp.int32)
    return found


def same_request(frame, other, table, requests, frames):
    inside = jnp.logical_and(other >= 0, other < frames)
    same = request_of(other, table, requests) == request_of(frame, table, requests)
    return jnp.logical_and(inside, same)


def attend_block(q_ref, k_ref, v_ref, largest, total, acc_in, acc_out):
    heads = q_ref.shape[1] // HD
    scale = 1.0 / math.sqrt(HD)
    maxima, sums = [], []
    for h in range(heads):
        cols = slice(h * HD, (h + 1) * HD)
        scores = lax.dot_general(
            k_ref[:, cols], q_ref[:, cols], (((1,), (1,)), ((), ())), preferred_element_type=F32
        )
        before = largest[h : h + 1]
        after = jnp.maximum(before, jnp.max(scores, axis=0, keepdims=True))
        weights = jnp.exp((scores - after) * scale)
        factor = jnp.exp((before - after) * scale)
        sums.append(total[h : h + 1] * factor + jnp.sum(weights, axis=0, keepdims=True))
        maxima.append(after)
        product = lax.dot_general(
            v_ref[:, cols], weights.astype(BF16), (((0,), (0,)), ((), ())),
            preferred_element_type=F32,
        )
        acc_out[cols, :] = acc_in[cols, :] * factor + product
    return jnp.concatenate(maxima, axis=0), jnp.concatenate(sums, axis=0)


def attend_kernel(offsets, requests, frames, table, qkv, *rest):
    count_in = 2 * (len(offsets) - 1)
    sources = ((qkv.at[1], qkv.at[2]),) + tuple(zip(rest[:count_in:2], rest[1:count_in:2]))
    acc, largest, total, q_buf, kv_buf, q_sem, kv_sem = rest[count_in:]
    mine, sign = table[2 * requests], table[2 * requests + 1]
    q_copy = pltpu.make_async_copy(qkv.at[0], q_buf, q_sem)
    q_copy.start()
    count = jnp.int32(0)
    for off, src in zip(offsets, sources):
        wanted = same_request(mine, mine + off * sign, table, requests, frames)

        @pl.when(wanted)
        def _(src=src, slot=count):
            pltpu.make_async_copy(src[0], kv_buf.at[slot, 0], kv_sem.at[slot, 0]).start()
            pltpu.make_async_copy(src[1], kv_buf.at[slot, 1], kv_sem.at[slot, 1]).start()

        count = count + wanted.astype(jnp.int32)
    acc[...] = jnp.zeros_like(acc)
    largest[...] = jnp.full(largest.shape, NEG_FILL, F32)
    total[...] = jnp.zeros_like(total)
    q_copy.wait()

    def step(i, carry):
        pltpu.make_async_copy(qkv.at[1], kv_buf.at[i, 0], kv_sem.at[i, 0]).wait()
        pltpu.make_async_copy(qkv.at[2], kv_buf.at[i, 1], kv_sem.at[i, 1]).wait()
        m, l = attend_block(
            q_buf, kv_buf.at[i, 0], kv_buf.at[i, 1], largest[...], total[...], acc, acc
        )
        largest[...] = m
        total[...] = l
        return carry

    lax.fori_loop(0, count, step, 0)


def finish_kernel(
    offset, requests, frames, seq, nrows,
    table, step_size, qkv, last_k, last_v, acc, largest, total, w_own, w_other, stream,
    scale, shift, fw, latent,
    new_latent, send,
    att, mixed, acc2, q_buf, kv_buf, w_buf, sems,
):
    mine, sign, place = table[2 * requests], table[2 * requests + 1], table[2 * requests + 2]
    wanted = same_request(mine, mine + offset * sign, table, requests, frames)
    heads = q_buf.shape[1] // HD
    half = heads // 2
    copies = [
        pltpu.make_async_copy(qkv.at[0], q_buf, sems.at[0]),
        pltpu.make_async_copy(last_k, kv_buf.at[0], sems.at[1]),
        pltpu.make_async_copy(last_v, kv_buf.at[1], sems.at[2]),
    ]
    w_copy = pltpu.make_async_copy(w_other, w_buf, sems.at[3])

    @pl.when(wanted)
    def _():
        for copy in copies:
            copy.start()

    w_copy.start()

    def store(source, row_sum):
        inverse = 1.0 / row_sum
        for h in range(heads):
            cols = slice(h * HD, (h + 1) * HD)
            inside = slice((h % half) * HD, (h % half + 1) * HD)
            att[h // half, :, inside] = (source[cols, :] * inverse[h : h + 1]).T.astype(BF16)

    @pl.when(wanted)
    def _():
        for copy in copies:
            copy.wait()
        _, row_sum = attend_block(
            q_buf, kv_buf.at[0], kv_buf.at[1], largest[...], total[...], acc, acc2
        )
        store(acc2, row_sum)

    @pl.when(jnp.logical_not(wanted))
    def _():
        store(acc, total[...])

    width = mixed.shape[1]
    tile = 512 if width % 512 == 0 else width
    rows = mixed.shape[0]
    w_copy.wait()

    def project(i, running):
        cols = pl.ds(pl.multiple_of(i * tile, tile), tile)
        value = (
            jnp.dot(att[place], w_own[:, cols], preferred_element_type=F32)
            + jnp.dot(att[1 - place], w_buf[:, cols], preferred_element_type=F32)
            + stream[:, cols].astype(F32)
        )
        mixed[:, cols] = value
        return running + jnp.sum(value, axis=1, keepdims=True)

    summed = lax.fori_loop(0, width // tile, project, jnp.zeros((rows, 1), F32))
    average = summed * (1.0 / width)
    squares = jnp.zeros((rows, 1), F32)
    for i in range(width // tile):
        centred = mixed[:, i * tile : (i + 1) * tile] - average
        squares = squares + jnp.sum(centred * centred, axis=1, keepdims=True)
    inverse = 1.0 / jnp.sqrt(squares * (1.0 / width) + EPSILON)
    velocity = jnp.zeros(new_latent.shape, F32)
    for i in range(width // tile):
        cols = slice(i * tile, (i + 1) * tile)
        normed = (mixed[:, cols] - average) * inverse
        modulated = (normed * (1.0 + scale[:, cols]) + shift[:, cols]).astype(BF16)
        velocity = velocity + lax.dot_general(
            fw[:, cols], modulated, (((1,), (1,)), ((), ())), preferred_element_type=F32
        )
    updated = latent[...] + step_size[0] * velocity
    new_latent[...] = updated

    column = lax.broadcasted_iota(jnp.int32, (LATC, F_TOK), 1) % PCOLS
    pieces = []
    for i in range(2):
        even = updated[2 * i * LATC : (2 * i + 1) * LATC]
        odd = updated[(2 * i + 1) * LATC : (2 * i + 2) * LATC]
        pieces.append(jnp.where(column == 0, 0.0, pltpu.roll(odd, 1, 1)))
        pieces.append(even)
        pieces.append(odd)
        pieces.append(jnp.where(column == PCOLS - 1, 0.0, pltpu.roll(even, F_TOK - 1, 1)))
    spread = jnp.concatenate(pieces, axis=0).T
    lower = lax.broadcasted_iota(jnp.int32, (PCOLS, 8 * LATC), 1) < 4 * LATC
    blank = jnp.zeros((PCOLS, 8 * LATC), F32)
    patch = [spread[r * PCOLS : (r + 1) * PCOLS] for r in range(PROWS)]
    for s in range(seq):
        first = (s * LROWS // seq) // 2
        for k in range(nrows):
            send[s, k * PCOLS : (k + 1) * PCOLS, :] = patch[first + k].astype(BF16)
        below = patch[first + nrows] if first + nrows < PROWS else blank
        above = patch[first - 1] if first > 0 else blank
        edge = jnp.where(lower, below, above)
        send[s, nrows * PCOLS : (nrows + 1) * PCOLS, :] = edge.astype(BF16)


def arrange_kernel(
    requests, table, own, other, bias_own, bias_other, up_own, up_other, out, bias, up
):
    place = table[2 * requests + 2]
    width = up.shape[1]
    hidden = up_own.shape[0]
    cols = pl.ds(pl.multiple_of(place * width, width), width)
    up[0:hidden] = up_own[:, cols]
    up[hidden : 2 * hidden] = up_other[:, cols]
    bias[...] = jnp.concatenate([bias_own[...], bias_other[...]] * 2, axis=1)
    out[...] = jnp.zeros_like(out)
    block = 4 * LATC
    outputs = own.shape[4]
    for parity in range(2):
        taps = ((0, 0, 1), (0, 1, 2), (1, 1, 0)) if parity == 0 else ((0, 0, 0), (0, 1, 1), (1, 0, 2))
        for a in range(3):
            for blk, half, b in taps:
                base = ((a * 2 + blk) * 2 + half) * block
                for jj in range(2):
                    for e in range(3):
                        rows = slice(base + (e + jj) * LATC, base + (e + jj + 1) * LATC)
                        at = jj * 2 * outputs
                        out[parity, rows, at : at + outputs] = own[a, b, e]
                        out[parity, rows, at + outputs : at + 2 * outputs] = other[a, b, e]


def decode_kernel(
    requests, frames, seq, slab, nrows,
    table, own, other, kernel, bias, up, up_bias,
    out,
    video, lhs, pixels,
):
    place, row_place = table[2 * requests + 2], table[2 * requests + 3]
    for s in range(seq):
        video[2 * s + place] = own[s]
        video[2 * s + 1 - place] = other[s]
    width = out.shape[3]
    hidden = up.shape[0] // 2
    owner = [request_of(f, table, requests) for f in range(frames)]
    blank = jnp.zeros((PCOLS, 8 * LATC), BF16)

    def tile_of(frame, k):
        return video[frame, k * PCOLS : (k + 1) * PCOLS, :]

    parities = (0, 1) if slab % 2 == 0 else (None,)
    for group, parity in enumerate(parities):
        for f in range(frames):
            for k in range(nrows):
                rows = slice((f * nrows + k) * PCOLS, (f * nrows + k + 1) * PCOLS)
                if parity is None:
                    beside = nrows
                elif parity == 0:
                    beside = k - 1 if k > 0 else nrows
                else:
                    beside = k + 1
                for a in range(3):
                    g = f - 2 + a
                    for blk, k_in in enumerate((k, beside)):
                        at = (a * 2 + blk) * 8 * LATC
                        value = blank
                        if g >= 0:
                            value = tile_of(g, k_in)
                            if a < 2:
                                value = jnp.where(owner[g] == owner[f], value, blank)
                        lhs[group, rows, at : at + 8 * LATC] = value
        which = lax.rem(row_place, 2) if parity is None else parity
        dense = jnp.dot(lhs[group], kernel[which], preferred_element_type=F32) + bias[...]
        act = (dense * (1.0 / (1.0 + jnp.exp(-dense)))).astype(BF16)
        for jj in range(2):
            part = act[:, jj * 2 * hidden : (jj + 1) * 2 * hidden]
            shared = jnp.dot(part, up[...], preferred_element_type=F32) + up_bias[...]
            for f in range(frames):
                alive = table[requests + owner[f]].astype(F32)
                for k in range(nrows):
                    rows = slice((f * nrows + k) * PCOLS, (f * nrows + k + 1) * PCOLS)
                    y = k if parity is None else 2 * k + parity
                    start = (f * slab + y) * LCOLS + jj
                    value = shared[rows] * alive
                    for lanes in range(width // HD):
                        at = slice(lanes * HD, (lanes + 1) * HD)
                        pixels[lanes, pl.ds(start, PCOLS, stride=2), :] = value[:, at]
    for f in range(frames):
        for y in range(slab):
            start = (f * slab + y) * LCOLS
            for lanes in range(width // HD):
                at = slice(lanes * HD, (lanes + 1) * HD)
                out[f, y, :, at] = pixels[lanes, start : start + LCOLS, :].astype(BF16)


def on_device(
    qkv,
    stream,
    out_weight,
    mod_scale,
    mod_shift,
    final_weight,
    latent,
    step_size,
    frame_counts,
    finished,
    conv_weight,
    conv_bias,
    up_weight,
    up_bias,
):
    seq, cores = lax.axis_size("seq"), lax.axis_size("tp")
    row_place, place = lax.axis_index("seq"), lax.axis_index("tp")
    tokens = qkv.shape[1]
    assert tokens == F_TOK and cores == 2
    requests = frame_counts.shape[1]
    frames = seq * cores
    reach = frames // 2 - 1
    hops = (reach - 1) // 2
    assert reach == 2 * hops + 1
    model = qkv.shape[3]
    both = ("seq", "tp")
    outward = [(2 * z + 1, 2 * z + 3) for z in range(seq - 1)]
    outward += [(2 * z + 2, 2 * z) for z in range(seq - 1)]
    inward = [(2 * z, 2 * z + 2) for z in range(seq - 1)]
    inward += [(2 * z + 3, 2 * z + 1) for z in range(seq - 1)]
    across = [(2 * z + 1, 2 * z + 2) for z in range(seq - 1)]
    across += [(2 * z + 2, 2 * z + 1) for z in range(seq - 1)]
    swap = [(0, 1), (1, 0)]

    table = jnp.concatenate(
        [
            frame_counts[0],
            finished[0],
            jnp.stack([row_place * 2 + place, 1 - 2 * place, place, row_place]).astype(jnp.int32),
        ]
    )
    stacked = qkv[0].transpose(1, 0, 2)
    chains = [(stacked[1],) * 2, (stacked[2],) * 2]
    swapped = [lax.ppermute(value, "tp", swap) for value in (stacked[1], stacked[2])]
    sources, offsets = [tuple(swapped)], [0, 1]
    for h in range(1, hops + 1):
        chains = [
            (lax.ppermute(out_chain, both, outward), lax.ppermute(in_chain, both, inward))
            for out_chain, in_chain in chains
        ]
        for which in range(2):
            arrived = tuple(chain[which] for chain in chains)
            sources += [arrived, tuple(lax.ppermute(value, "tp", swap) for value in arrived)]
        offsets += [2 * h, -(2 * h - 1), -2 * h, 2 * h + 1]
    last = [lax.ppermute(chain[0], both, across) for chain in chains]

    w_other = lax.ppermute(out_weight, "tp", swap)
    conv_other = lax.ppermute(conv_weight, "tp", swap)
    bias_other = lax.ppermute(conv_bias[None], "tp", swap)
    up_other = lax.ppermute(up_weight, "tp", swap)
    out_width = up_bias.shape[0]

    arranged, bias, up = pl.pallas_call(
        functools.partial(arrange_kernel, requests),
        name="arrange",
        out_shape=(
            jax.ShapeDtypeStruct((2, 48 * LATC, 4 * conv_weight.shape[4]), BF16),
            jax.ShapeDtypeStruct((1, 4 * conv_weight.shape[4]), F32),
            jax.ShapeDtypeStruct((2 * up_weight.shape[0], out_width), BF16),
        ),
        in_specs=[SMEM] + [VMEM] * 6,
        out_specs=(VMEM,) * 3,
        compiler_params=pltpu.CompilerParams(vmem_limit_bytes=8 * MIB),
    )(table, conv_weight, conv_other, conv_bias[None], bias_other, up_weight, up_other)

    slots = frames // 2
    acc, largest, total = pl.pallas_call(
        functools.partial(attend_kernel, tuple(offsets), requests, frames),
        name="attend",
        out_shape=(
            jax.ShapeDtypeStruct((model, tokens), F32),
            jax.ShapeDtypeStruct((model // HD, tokens), F32),
            jax.ShapeDtypeStruct((model // HD, tokens), F32),
        ),
        in_specs=[SMEM] + [ANY] * (1 + 2 * len(sources)),
        out_specs=(VMEM, VMEM, VMEM),
        scratch_shapes=[
            pltpu.VMEM((tokens, model), BF16),
            pltpu.VMEM((slots, 2, tokens, model), BF16),
            pltpu.SemaphoreType.DMA,
            pltpu.SemaphoreType.DMA((slots, 2)),
        ],
        compiler_params=pltpu.CompilerParams(vmem_limit_bytes=(slots + 8) * MIB),
    )(table, stacked, *[value for source in sources for value in source])
    acc, arranged, bias, up = lax.optimization_barrier((acc, arranged, bias, up))

    slab = LROWS // seq
    assert slab == 1 or slab % 2 == 0
    nrows = (slab + 1) // 2
    width = stream.shape[2]
    patch = final_weight.shape[1]
    new_latent, send = pl.pallas_call(
        functools.partial(finish_kernel, -reach, requests, frames, seq, nrows),
        name="finish",
        out_shape=(
            jax.ShapeDtypeStruct((patch, tokens), F32),
            jax.ShapeDtypeStruct((seq, (nrows + 1) * PCOLS, 8 * LATC), BF16),
        ),
        in_specs=[SMEM, SMEM, ANY, ANY, ANY] + [VMEM] * 4 + [ANY] + [VMEM] * 5,
        out_specs=(VMEM, VMEM),
        scratch_shapes=[
            pltpu.VMEM((2, tokens, model // 2), BF16),
            pltpu.VMEM((tokens, width), F32),
            pltpu.VMEM((model, tokens), F32),
            pltpu.VMEM((tokens, model), BF16),
            pltpu.VMEM((2, tokens, model), BF16),
            pltpu.VMEM(out_weight.shape, BF16),
            pltpu.SemaphoreType.DMA((4,)),
        ],
        compiler_params=pltpu.CompilerParams(vmem_limit_bytes=32 * MIB),
    )(
        table,
        step_size,
        stacked,
        last[0],
        last[1],
        acc,
        largest,
        total,
        out_weight,
        w_other,
        stream[0],
        mod_scale,
        mod_shift,
        final_weight.T,
        latent[0].T,
    )

    received = lax.all_to_all(send, "seq", split_axis=0, concat_axis=0, tiled=True)
    received_other = lax.ppermute(received, "tp", swap)
    decoded = pl.pallas_call(
        functools.partial(decode_kernel, requests, frames, seq, slab, nrows),
        name="decode",
        out_shape=jax.ShapeDtypeStruct((frames, slab, LCOLS, out_width), BF16),
        in_specs=[SMEM] + [VMEM] * 6,
        out_specs=VMEM,
        scratch_shapes=[
            pltpu.VMEM((frames, (nrows + 1) * PCOLS, 8 * LATC), BF16),
            pltpu.VMEM((2 if slab % 2 == 0 else 1, frames * nrows * PCOLS, 48 * LATC), BF16),
            pltpu.VMEM((out_width // HD, frames * slab * LCOLS, HD), F32),
        ],
        compiler_params=pltpu.CompilerParams(vmem_limit_bytes=24 * MIB),
    )(
        table,
        received,
        received_other,
        arranged,
        bias,
        up,
        up_bias[None],
    )
    return (new_latent.T[None], decoded[None])


def solution(mesh):
    in_specs = (
        P(("groups", "section"), ("seq", "tp"), None, None),
        P(("groups", "section"), ("seq", "tp"), None),
        P("tp", None),
        P(("groups", "section"), None),
        P(("groups", "section"), None),
        P(),
        P(("groups", "section"), ("seq", "tp"), None),
        P(("groups", "section")),
        P(("groups", "section"), None),
        P(("groups", "section"), None),
        P(None, None, None, None, "tp"),
        P("tp"),
        P("tp", None),
        P("tp"),
    )
    out_specs = (
        P(("groups", "section"), ("seq", "tp"), None),
        P(("groups", "section"), None, "seq", None, "tp"),
    )
    return jax.shard_map(
        on_device, mesh=mesh, in_specs=in_specs, out_specs=out_specs, check_vma=False
    )
```
